32 devices in a mesh: group: 2 (over y), tile: 8 (over z, x), strip: 2 (over core).
Axes of the slice: x: 2, y: 2, z: 4, core: 2. Of those that a mesh axis runs over, the one named last changes fastest.
Arguments:
- image: bfloat16 [128, 256, 256], P(('group', 'strip'), 'tile'), parts along dimension 0, may hold values from -16 to 16
- bn_gain: float32 [256], replicated, may hold values from 0.25 to 1.75
- bn_shift: float32 [256], replicated, may hold values from -3 to 3
- w_expand: bfloat16 [256, 1024], replicated, may hold values from -0.375 to 0.375
- b_expand: float32 [1024], replicated, may hold values from -3 to 3
- w_depth: float32 [9, 1024], replicated, may hold values from -2 to 2
- b_depth: float32 [1024], replicated, may hold values from -3 to 3
- w_project: bfloat16 [1024, 256], replicated, may hold values from -0.1875 to 0.1875
- b_project: float32 [256], replicated, may hold values from -3 to 3
- attn_gain: float32 [256], replicated, may hold values from 0.25 to 1.75
- attn_shift: float32 [256], replicated, may hold values from -2 to 2
- w_qkv: bfloat16 [256, 768], replicated, may hold values from -0.375 to 0.375
- w_out: bfloat16 [256, 256], replicated, may hold values from -0.375 to 0.375
- rel_table: float32 [8, 225], replicated, may hold values from -4 to 304
- ffn_gain: float32 [256], replicated, may hold values from 0.25 to 1.75
- ffn_shift: float32 [256], replicated, may hold values from -2 to 2
- w_up: bfloat16 [256, 1024], replicated, may hold values from -0.375 to 0.375
- b_up: float32 [1024], replicated, may hold values from -3 to 3
- w_down: bfloat16 [1024, 256], replicated, may hold values from -0.1875 to 0.1875
- b_down: float32 [256], replicated, may hold values from -3 to 3
Outputs:
- block_out: bfloat16 [128, 256, 256], P(('group', 'strip'), 'tile'), parts along dimension 0
The draws below stay inside these ranges and needn't reach their ends.
There are 2 independent parts, one for each index of `group`. The reference program is written for one: setup_inputs(seed, part) draws one part's arguments, and reference() takes and returns one part's arrays. A program takes and returns all parts, laid end to end along the dimension named above; an argument that names none is the same for every part. Nothing has to cross between parts.
All inputs are finite; a program needn't handle non-finite values.
Results may differ from the reference program's by a relative error of at most 0.0064.
Values may be sent and summed in bfloat16 or wider, within the bound.
A program may use at most 64 MiB of HBM per device.

```python
import math
import jax
import jax.numpy as jnp
from jax import lax

C = 256
E = 1024
F = 1024
GRID = 8
TW = 32
HEADS = 8
H = 64
W = 256


def draw_image(key, part):
    key_noise = jax.random.fold_in(key, 11)
    key_token = jax.random.fold_in(key, 12)
    key_channel = jax.random.fold_in(key, 13)
    low_log = math.log(0.3)
    high_log = math.log(3.0)
    chan_scale = jnp.exp(jax.random.uniform(key_channel, (C,), jnp.float32, low_log, high_log))
    token_scale = jnp.exp(jax.random.uniform(key_token, (H, W, 1), jnp.float32, low_log, high_log))
    noise = jax.random.normal(key_noise, (H, W, C), jnp.float32)
    pixels = noise * token_scale * chan_scale
    return jnp.clip(pixels, -16.0, 16.0).astype(jnp.bfloat16)


def draw_rel_table(key, part):
    entries = (2 * GRID - 1) ** 2
    key_base = jax.random.fold_in(key, 21)
    base_table = jnp.clip(jax.random.normal(key_base, (HEADS, entries), jnp.float32), -4.0, 4.0)
    return base_table.astype(jnp.float32)


def gaussian(own_key, dims, scale, limit, held_as=jnp.bfloat16):
    return jnp.clip(scale * jax.random.normal(own_key, dims, jnp.float32), -limit, limit).astype(held_as)


def setup_inputs(seed: int = 0, part: int = 0) -> dict:
    keys = jax.random.split(jax.random.key(seed), 21)
    part_keys = jax.random.split(jax.random.fold_in(keys[20], part), 21)
    return {
        "image": draw_image(jax.random.fold_in(jax.random.fold_in(keys[20], part), 71), part),
        "bn_gain": jnp.clip(1.0 + 0.15 * jax.random.normal(keys[1], (C,), jnp.float32), 0.25, 1.75),
        "bn_shift": gaussian(keys[2], (C,), 0.5, 3.0, jnp.float32),
        "w_expand": gaussian(keys[3], (C, E), C ** -0.5, 0.375),
        "b_expand": gaussian(keys[4], (E,), 0.5, 3.0, jnp.float32),
        "w_depth": gaussian(keys[5], (9, E), 9 ** -0.5, 2.0, jnp.float32),
        "b_depth": gaussian(keys[6], (E,), 0.5, 3.0, jnp.float32),
        "w_project": gaussian(keys[7], (E, C), E ** -0.5, 0.1875),
        "b_project": gaussian(keys[8], (C,), 0.5, 3.0, jnp.float32),
        "attn_gain": jnp.clip(1.0 + 0.15 * jax.random.normal(keys[9], (C,), jnp.float32), 0.25, 1.75),
        "attn_shift": gaussian(keys[10], (C,), 0.3, 2.0, jnp.float32),
        "w_qkv": gaussian(keys[11], (C, 3 * C), C ** -0.5, 0.375),
        "w_out": gaussian(keys[12], (C, C), C ** -0.5, 0.375),
        "rel_table": draw_rel_table(jax.random.fold_in(keys[20], 71), part),
        "ffn_gain": jnp.clip(1.0 + 0.15 * jax.random.normal(keys[14], (C,), jnp.float32), 0.25, 1.75),
        "ffn_shift": gaussian(keys[15], (C,), 0.3, 2.0, jnp.float32),
        "w_up": gaussian(keys[16], (C, F), C ** -0.5, 0.375),
        "b_up": gaussian(keys[17], (F,), 0.5, 3.0, jnp.float32),
        "w_down": gaussian(keys[18], (F, C), F ** -0.5, 0.1875),
        "b_down": gaussian(keys[19], (C,), 0.5, 3.0, jnp.float32),
    }


EPSILON = 1e-05

def gelu_tanh(inputs):
    return jax.nn.gelu(inputs, approximate=True)

def layer_norm(inputs, norm_gain, norm_shift):
    center = lax.optimization_barrier(jnp.mean(inputs, axis=-1, keepdims=True))
    spread = lax.optimization_barrier(jnp.mean(jnp.square(inputs - center), axis=-1, keepdims=True))
    return (inputs - center) * lax.rsqrt(spread + EPSILON) * norm_gain + norm_shift

def expand_tokens(pixels, bn_gain, bn_shift, w_expand, b_expand):
    normed = (pixels.astype(jnp.float32) * bn_gain + bn_shift).astype(jnp.bfloat16)
    pre_act = jnp.dot(normed, w_expand, preferred_element_type=jnp.float32) + b_expand
    return gelu_tanh(pre_act).astype(jnp.bfloat16)

def depthwise(framed, w_depth, b_depth):
    out_rows = framed.shape[0] - 2
    out_cols = framed.shape[1] - 2
    accum_sum = jnp.zeros((out_rows, out_cols, framed.shape[2]), jnp.float32) + b_depth
    for row_step in range(3):
        for col_step in range(3):
            window_part = framed[row_step:row_step + out_rows, col_step:col_step + out_cols]
            accum_sum = accum_sum + window_part.astype(jnp.float32) * w_depth[row_step * 3 + col_step]
    return gelu_tanh(accum_sum).astype(jnp.bfloat16)

def position_bias(rel_table):
    grid_side = GRID
    token_ids = jnp.arange(grid_side * grid_side, dtype=jnp.int32)
    row_of = token_ids // grid_side
    col_of = token_ids % grid_side
    offset = (row_of[:, None] - row_of[None, :] + grid_side - 1) * (2 * grid_side - 1) + (col_of[:, None] - col_of[None, :] + grid_side - 1)
    entry_ids = jnp.arange((2 * grid_side - 1) ** 2, dtype=jnp.int32)
    onehot = (offset.reshape(-1)[:, None] == entry_ids[None, :]).astype(jnp.float32)
    pos_bias = jnp.dot(rel_table, onehot.T, precision=lax.Precision.HIGHEST, preferred_element_type=jnp.float32)
    return pos_bias.reshape(rel_table.shape[0], grid_side * grid_side, grid_side * grid_side)

def grid_attention(windows, attn_gain, attn_shift, w_qkv, w_out, pos_bias):
    win_count = windows.shape[0]
    places = windows.shape[1]
    model_width = windows.shape[2]
    head_count = pos_bias.shape[0]
    head_size = model_width // head_count
    normed = layer_norm(windows.astype(jnp.float32), attn_gain, attn_shift).astype(jnp.bfloat16)
    projected_qkv = jnp.dot(normed, w_qkv, preferred_element_type=jnp.float32)
    queries = (projected_qkv[..., :model_width] * head_size ** (-0.5)).astype(jnp.bfloat16)
    key_heads = projected_qkv[..., model_width:2 * model_width].astype(jnp.bfloat16)
    value_heads = projected_qkv[..., 2 * model_width:].astype(jnp.bfloat16)
    queries = queries.reshape(win_count, places, head_count, head_size).astype(jnp.float32)
    key_heads = key_heads.reshape(win_count, places, head_count, head_size).astype(jnp.float32)
    value_heads = value_heads.reshape(win_count, places, head_count, head_size).astype(jnp.float32)
    scores = jnp.einsum('wihd,wjhd->whij', queries, key_heads, precision=lax.Precision.HIGHEST) + pos_bias[None]
    row_peak = lax.optimization_barrier(jnp.max(scores, axis=-1, keepdims=True))
    exp_scores = jnp.exp(scores - row_peak)
    weights_bf = (exp_scores / lax.optimization_barrier(jnp.sum(exp_scores, axis=-1, keepdims=True))).astype(jnp.bfloat16)
    context = jnp.einsum('whij,wjhd->wihd', weights_bf.astype(jnp.float32), value_heads, precision=lax.Precision.HIGHEST)
    context = context.astype(jnp.bfloat16).reshape(win_count, places, model_width)
    attended = windows.astype(jnp.float32) + jnp.dot(context, w_out, preferred_element_type=jnp.float32)
    return attended.astype(jnp.bfloat16)

def feed_forward(tokens_in, ffn_gain, ffn_shift, w_up, b_up, w_down, b_down):
    normed = layer_norm(tokens_in.astype(jnp.float32), ffn_gain, ffn_shift).astype(jnp.bfloat16)
    hidden = gelu_tanh(jnp.dot(normed, w_up, preferred_element_type=jnp.float32) + b_up).astype(jnp.bfloat16)
    result = tokens_in.astype(jnp.float32) + jnp.dot(hidden, w_down, preferred_element_type=jnp.float32) + b_down
    return result.astype(jnp.bfloat16)

def reference(image, bn_gain, bn_shift, w_expand, b_expand, w_depth, b_depth, w_project, b_project, attn_gain, attn_shift, w_qkv, w_out, rel_table, ffn_gain, ffn_shift, w_up, b_up, w_down, b_down):
    height = image.shape[0]
    width_all = image.shape[1]
    channels = image.shape[2]
    blocks = width_all // TW
    padded = jnp.pad(image, ((0, 0), (1, 1), (0, 0)))

    def column_block(block_at):
        start_col = (block_at * TW).astype(jnp.int32)
        window_cols = lax.dynamic_slice_in_dim(padded, start_col, TW + 2, 1)
        expanded = expand_tokens(window_cols, bn_gain, bn_shift, w_expand, b_expand)
        col_index = start_col - 1 + jnp.arange(TW + 2, dtype=jnp.int32)
        inside = (col_index >= 0) & (col_index < width_all)
        expanded = jnp.where(inside[None, :, None], expanded, jnp.zeros((), jnp.bfloat16))
        expanded = jnp.pad(expanded, ((1, 1), (0, 0), (0, 0)))
        hidden = depthwise(expanded, w_depth, b_depth)
        projected = jnp.dot(hidden, w_project, preferred_element_type=jnp.float32) + b_project
        return (window_cols[:, 1:-1].astype(jnp.float32) + projected).astype(jnp.bfloat16)
    section_one = lax.map(column_block, jnp.arange(blocks, dtype=jnp.int32))
    section_one = section_one.transpose(1, 0, 2, 3).reshape(height, width_all, channels)
    across = height // GRID
    along_cols = width_all // GRID
    windows = section_one.reshape(GRID, across, GRID, along_cols, channels).transpose(1, 3, 0, 2, 4)
    total_windows = across * along_cols
    windows = windows.reshape(total_windows, GRID * GRID, channels)
    pos_bias = position_bias(rel_table)
    per_block = math.gcd(total_windows, 64)
    grouped = windows.reshape(total_windows // per_block, per_block, GRID * GRID, channels)

    def window_block(window_group):
        attended = grid_attention(window_group, attn_gain, attn_shift, w_qkv, w_out, pos_bias)
        return feed_forward(attended, ffn_gain, ffn_shift, w_up, b_up, w_down, b_down)
    result = lax.map(window_block, grouped)
    result = result.reshape(across, along_cols, GRID, GRID, channels).transpose(2, 0, 3, 1, 4)
    return result.reshape(height, width_all, channels)
```

```python
import functools
import math

import jax
import jax.numpy as jnp
from jax import lax
from jax.experimental import pallas as pl
from jax.experimental.pallas import tpu as pltpu
from jax.sharding import PartitionSpec as P

GRID = 8
EPSILON = 1e-05
LANES = 128
PACK = 16
PAD = 8
FAR = -1e6
MESH = pl.DeviceIdType.MESH

ROOT = math.sqrt(2.0 / math.pi)
SCALE = (ROOT * 0.044715) ** (1.0 / 3.0)
INNER = ROOT / SCALE
UNSCALE = 0.5 / SCALE
LOG2E = math.log2(math.e)


def scaled_gelu(z):
    return z + z * jnp.tanh(z * (z * z + INNER))


def layer_norm(inputs, norm_gain, norm_shift):
    center = jnp.mean(inputs, axis=-1, keepdims=True)
    spread = jnp.mean(jnp.square(inputs - center), axis=-1, keepdims=True)
    return (inputs - center) * lax.rsqrt(spread + EPSILON) * norm_gain + norm_shift


def dot(a, b):
    return jnp.dot(a, b, preferred_element_type=jnp.float32)


def dot_on(a, b, dims):
    return lax.dot_general(a, b, ((dims[:1], dims[1:]), ((), ())), preferred_element_type=jnp.float32)


def block_kernel(
    strips,
    col_groups,
    head_count,
    image_ref,
    bng_ref,
    bns_ref,
    wexp_ref,
    bexp_ref,
    wdep_ref,
    bdep_ref,
    wproj_hbm,
    bproj_ref,
    ag_ref,
    as_ref,
    wqkv_hbm,
    wout_hbm,
    table_ref,
    fg_ref,
    fs_ref,
    wup_hbm,
    bup_ref,
    wdown_hbm,
    bdown_ref,
    out_hbm,
    wproj_ref,
    wqkv_ref,
    wout_ref,
    wup_ref,
    wdown_ref,
    edge,
    cols_in,
    rows_in,
    xs,
    e_s,
    be_s,
    wd_s,
    h_s,
    sec,
    arr,
    tab_s,
    bias_s,
    swap_s,
    back_s,
    outb,
    sec2,
    ob,
    outv,
    wsem,
    send1,
    recv1,
    send2,
    recv2,
    hsend,
    hrecv,
    osem,
):
    bf, f32 = jnp.bfloat16, jnp.float32
    rows, cols, chans = image_ref.shape
    hidden = wexp_ref.shape[1]
    groups = cols // GRID
    width = cols + 2 * PAD
    peers = strips * GRID
    kinds = strips + 2
    span = peers * PACK
    mine = GRID // strips
    places = GRID * GRID
    head_size = chans // head_count
    halves = chans // LANES
    half_heads = LANES // head_size
    me_s = lax.axis_index("strip")
    tile = lax.axis_index("tile")
    me_k = tile // col_groups
    within = tile % col_groups
    me_u = me_s * GRID + me_k

    def device(s, k):
        return {"strip": s, "tile": k * col_groups + within}

    barrier = pltpu.get_barrier_semaphore()
    for m in range(1, peers):
        s, k = (me_s + m // GRID) % strips, (me_k + m) % GRID
        pl.semaphore_signal(barrier, inc=1, device_id=device(s, k), device_id_type=MESH)
    tiles = GRID * col_groups
    sides = ((tile + tiles - 1) % tiles, (tile + 1) % tiles)
    for t in sides:
        for s in range(strips):
            pl.semaphore_signal(
                barrier, inc=1, device_id={"strip": s, "tile": t}, device_id_type=MESH
            )

    weights = [
        pltpu.make_async_copy(src, dst, wsem.at[i])
        for i, (src, dst) in enumerate(
            (
                (wproj_hbm, wproj_ref),
                (wqkv_hbm, wqkv_ref),
                (wout_hbm, wout_ref),
                (wup_hbm, wup_ref),
                (wdown_hbm, wdown_ref),
            )
        )
    ]
    for copy in weights:
        copy.start()

    def put(at, value):
        for f in range(halves):
            xs[f, at, :] = value[:, LANES * f : LANES * (f + 1)]

    def take(at, count, stride):
        return jnp.concatenate(
            [xs[f, pl.ds(at, count, stride=stride), :] for f in range(halves)], axis=1
        )

    @pl.loop(0, rows)
    def _(r):
        at = pl.multiple_of((r + 1) * width + PAD, PAD)
        put(pl.ds(at, cols), image_ref[r].astype(f32))

    edge[0] = take(width + PAD, rows, width).astype(bf)
    edge[1] = take(width + PAD + cols - 1, rows, width).astype(bf)

    pl.semaphore_wait(barrier, peers - 1 + 2 * strips)

    halo = []
    for i in range(2):
        halo.append(
            pltpu.make_async_remote_copy(
                image_ref.at[(rows - 1) * (1 - i)],
                rows_in.at[i],
                hsend.at[2, i],
                hrecv.at[2, i],
                device_id={"strip": (me_s + 1 + i * (strips - 2)) % strips, "tile": tile},
                device_id_type=MESH,
            )
        )
    for i in range(2):
        for s in range(strips):
            halo.append(
                pltpu.make_async_remote_copy(
                    edge.at[i],
                    cols_in.at[1 - i, me_s],
                    hsend.at[i, s],
                    hrecv.at[1 - i, me_s],
                    device_id={"strip": s, "tile": sides[i]},
                    device_id_type=MESH,
                )
            )
    for copy in halo:
        copy.start()

    row16 = lax.broadcasted_iota(jnp.int32, (PACK, 1), 0)
    bexp = jnp.broadcast_to(bexp_ref[...] * SCALE, (PACK, hidden))
    for kk in range(kinds):
        be = bexp
        if kk == 0:
            be = be + jnp.where(row16 == 0, jnp.where(me_s == 0, FAR, 0.0), 0.0)
        if kk == kinds - 1:
            be = be + jnp.where(
                row16 == PACK - 1, jnp.where(me_s == strips - 1, FAR, 0.0), 0.0
            )
        be_s[kk] = be.astype(bf)
    for tap in range(9):
        wd_s[tap] = jnp.broadcast_to(wdep_ref[tap : tap + 1, :] * 0.5, (PACK, hidden)).astype(bf)
    wd_s[9] = jnp.broadcast_to(bdep_ref[...] * SCALE, (PACK, hidden)).astype(bf)

    for i in range(2):
        pltpu.make_async_copy(rows_in.at[i], rows_in.at[i], hrecv.at[2, i]).wait()
        at = PAD + (rows + 1) * width * i
        put(pl.ds(at, cols), rows_in[i].astype(f32))

    bng = bng_ref[...] * SCALE
    bns = bns_ref[...] * SCALE
    step = strips * width

    def expand(first, count):
        @pl.loop(0, count)
        def _(q):
            at = first + 2 * q
            lhs = []
            for cc in range(2):
                for kk in range(kinds):
                    raw = take(kk * width + PAD - 1 + at + cc, PACK, step)
                    lhs.append((raw * bng + bns).astype(bf))
            lhs = jnp.concatenate(lhs, axis=0)
            for n in range(hidden // 256):
                lanes = slice(256 * n, 256 * (n + 1))
                z = dot(lhs, wexp_ref[:, lanes]).astype(bf)
                for cc in range(2):
                    for kk in range(kinds):
                        i = cc * kinds + kk
                        zi = z[PACK * i : PACK * (i + 1)] + be_s[kk, :, lanes]
                        e_s[at + cc, kk, :, lanes] = scaled_gelu(zi)

    expand(GRID, 1)

    def first_send(j):
        sends = []
        for m in order:
            s, k = (me_s + m // GRID) % strips, (me_k + m) % GRID
            sends.append(
                pltpu.make_async_remote_copy(
                    sec.at[j, s * GRID + k],
                    arr.at[j, me_u],
                    send1.at[j],
                    recv1.at[j],
                    device_id=device(s, k),
                    device_id_type=MESH,
                )
            )
        return sends, pltpu.make_async_copy(sec.at[j, me_u], arr.at[j, me_u], recv1.at[j])

    def back_send(j):
        sends = []
        for m in order:
            s, k = (me_s + m // GRID) % strips, (me_k + m) % GRID
            sends.append(
                pltpu.make_async_remote_copy(
                    outb.at[j, s * GRID + k],
                    sec2.at[j, me_u],
                    send2.at[j],
                    recv2.at[j],
                    device_id=device(s, k),
                    device_id_type=MESH,
                )
            )
        return sends, pltpu.make_async_copy(outb.at[j, me_u], sec2.at[j, me_u], recv2.at[j])

    half = GRID // 2
    order = [m for m in range(1, peers)]
    order.sort(key=lambda m: abs(m % GRID - half))

    def flag(ok):
        return jnp.broadcast_to(jnp.where(ok, 1.0, 0.0), (PACK, hidden)).astype(bf)

    for j in range(groups):
        start = (GRID * (j + 1) + 2) % (cols + 2)
        if j == groups - 2:
            for i in range(2):
                for s in range(strips):
                    pltpu.make_async_copy(cols_in.at[i, s], cols_in.at[i, s], hrecv.at[i, s]).wait()
            for i in range(2):
                at = PAD - 1 + (cols + 1) * i
                put(pl.ds(width + at, rows, stride=width), cols_in[i, me_s].astype(f32))
                above = cols_in[i, (me_s + strips - 1) % strips].astype(f32)
                put(pl.ds(at, 1), above[rows - 1 : rows])
                below = cols_in[i, (me_s + 1) % strips].astype(f32)
                low = (rows + 1) * width + at
                put(pl.ds(low, 1), below[0:1])
        expand(start, GRID // 2)
        if j == groups - 2:
            ok = flag(tile < tiles - 1)
            for kk in range(kinds):
                e_s[cols + 1, kk] = e_s[cols + 1, kk] * ok
        if j == groups - 1:
            ok = flag(tile > 0)
            for kk in range(kinds):
                e_s[0, kk] = e_s[0, kk] * ok
        base = GRID * ((j + 1) % groups)

        @pl.loop(0, GRID // 2)
        def _(q):
            for c in range(hidden // LANES):
                lanes = slice(LANES * c, LANES * (c + 1))
                taps = [wd_s[t, :, lanes] for t in range(10)]
                for cc in range(2):
                    at = base + 2 * q + cc
                    for kk in range(strips):
                        acc = taps[9]
                        for a in range(3):
                            for b in range(3):
                                acc = acc + e_s[at + b, kk + a, :, lanes] * taps[3 * a + b]
                        h_s[kk, 2 * q + cc, :, lanes] = scaled_gelu(acc)

        if j == 0:
            weights[0].wait()
        skip = jnp.concatenate(
            [
                take((kk + 1) * width + PAD + base + c, PACK, step)
                for kk in range(strips)
                for c in range(GRID)
            ],
            axis=0,
        )
        proj = dot(h_s[...].reshape(span, hidden), wproj_ref[...])
        out = skip + proj * UNSCALE + bproj_ref[...]
        sec[j] = out.astype(bf).reshape(peers, PACK, chans)
        sends, own = first_send(j)
        for copy in sends:
            copy.start()
        own.start()

    side = 2 * GRID - 1
    slot = 2 * GRID
    tab_s[...] = jnp.zeros_like(tab_s)
    tab_s[:, 0 : side * side] = table_ref[...] * LOG2E
    table = tab_s[...]
    lane = lax.broadcasted_iota(jnp.int32, (head_count, LANES), 1)
    sub = lax.broadcasted_iota(jnp.int32, (head_count, LANES), 0)
    in_pair = LANES // (half_heads * slot)
    for f in range(halves):
        keep = sub == half_heads * f + lane // slot % half_heads
        even, odd = [], []
        for d in range(side):
            x = pltpu.roll(table, (table.shape[1] - side * d) % table.shape[1], 1)[:, :LANES]
            x = jnp.where(lane < side, x, 0.0)
            n = slot
            while n < LANES:
                x = x + pltpu.roll(x, n, 1)
                n *= 2
            x = jnp.sum(jnp.where(keep, x, 0.0), axis=0, keepdims=True)
            x = jnp.broadcast_to(x, (GRID, LANES))
            x = pltpu.roll(x, LANES - (GRID - 1), 1, stride=1, stride_axis=0)
            even.append(x)
            odd.append(pltpu.roll(x, GRID, 1))
        lane8 = lax.broadcasted_iota(jnp.int32, (GRID, LANES), 1)
        first = lane8 % slot < GRID
        pair_of = lane8 // (half_heads * slot)
        tiles_by = []
        for d in range(side - 2 * in_pair + 1):
            tile_bias = jnp.where(first, even[d], odd[d + 1])
            for b in range(1, in_pair):
                more = jnp.where(first, even[d + 2 * b], odd[d + 2 * b + 1])
                tile_bias = jnp.where(pair_of == b, more, tile_bias)
            tiles_by.append(tile_bias)
        for g in range(GRID // 2 // in_pair):
            for r in range(GRID):
                bias_s[f, GRID * r : GRID * (r + 1), LANES * g : LANES * (g + 1)] = tiles_by[
                    GRID - 1 + 2 * in_pair * g - r
                ]

    row_id = lax.broadcasted_iota(jnp.int32, (span, span), 0)
    col_id = lax.broadcasted_iota(jnp.int32, (span, span), 1)

    def place_of(n):
        p = n % PACK
        s, k = n // PACK // GRID, n // PACK % GRID
        grid_row = (rows // GRID) * s + p // mine
        return p % mine * places + grid_row * GRID + k

    swap_s[...] = jnp.where(row_id == place_of(col_id), 1.0, 0.0).astype(bf)
    back_s[...] = jnp.where(col_id == place_of(row_id), 1.0, 0.0).astype(bf)
    lane16 = lax.broadcasted_iota(jnp.int32, (PACK, LANES), 1) // head_size
    masks = [jnp.where(lane16 == h, 1.0, 0.0).astype(bf) for h in range(half_heads)]
    weights[1].wait()
    weights[2].wait()
    pairs = places // PACK

    @pl.loop(0, groups)
    def _(j):
        pltpu.make_async_copy(arr.at[j], arr.at[j], recv1.at[j]).wait()
        x = arr[j].reshape(span, chans).astype(f32)
        normed = layer_norm(x, ag_ref[...], as_ref[...]).astype(bf)
        normed = dot(swap_s[...], normed).astype(bf)
        q = (dot(normed, wqkv_ref[:, 0:chans]) * (head_size**-0.5 * LOG2E)).astype(bf)
        key = dot(normed, wqkv_ref[:, chans : 2 * chans]).astype(bf)
        val = dot(normed, wqkv_ref[:, 2 * chans :]).astype(bf)
        ctx = []
        for w in range(mine):
            parts = []
            for f in range(halves):
                at = (slice(places * w, places * (w + 1)), slice(LANES * f, LANES * (f + 1)))
                qh, kh, vh = q[at], key[at], val[at]
                qbd = jnp.concatenate(
                    [
                        qh[PACK * b : PACK * (b + 1)] * masks[h]
                        for b in range(pairs)
                        for h in range(half_heads)
                    ],
                    axis=0,
                )
                s = dot_on(kh, qbd, (1, 1)) + bias_s[f]
                e = jnp.exp2(s - jnp.max(s, axis=0, keepdims=True))
                p = (e * (1.0 / jnp.sum(e, axis=0, keepdims=True))).astype(bf)
                o = dot_on(p, vh, (0, 0)).reshape(pairs, half_heads, PACK, LANES)
                pick = o[:, 0]
                here = lax.broadcasted_iota(jnp.int32, pick.shape, 2) // head_size
                for h in range(1, half_heads):
                    pick = jnp.where(here == h, o[:, h], pick)
                parts.append(pick.reshape(places, LANES).astype(bf))
            ctx.append(jnp.concatenate(parts, axis=1))
        ctx = dot(back_s[...], jnp.concatenate(ctx, axis=0)).astype(bf)
        attended = (x + dot(ctx, wout_ref[...])).astype(bf)
        outb[j] = attended.reshape(peers, PACK, chans)
        sends, own = back_send(j)
        for copy in sends:
            copy.start()
        own.start()

    weights[3].wait()
    weights[4].wait()

    @pl.loop(0, groups)
    def _(j):
        pltpu.make_async_copy(sec2.at[j], sec2.at[j], recv2.at[j]).wait()
        x = sec2[j].reshape(span, chans).astype(f32)
        normed = layer_norm(x, fg_ref[...] * SCALE, fs_ref[...] * SCALE).astype(bf)
        bup = jnp.broadcast_to(bup_ref[...] * SCALE, (PACK, hidden)).astype(bf)
        for n in range(hidden // 256):
            lanes = slice(256 * n, 256 * (n + 1))
            z = dot(normed, wup_ref[:, lanes]).astype(bf).reshape(strips, GRID, PACK, 256)
            h_s[:, :, :, lanes] = scaled_gelu(z + bup[:, lanes])
        res = dot(h_s[...].reshape(span, hidden), wdown_ref[...]) * UNSCALE
        res = x + res + bdown_ref[...]
        for kk in range(strips):
            for c in range(GRID):
                i = kk * GRID + c
                for f in range(halves):
                    ob[f, pl.ds(i, PACK, stride=peers), :] = res[
                        PACK * i : PACK * (i + 1), LANES * f : LANES * (f + 1)
                    ]
        outv[j] = jnp.concatenate(
            [ob[f].astype(bf).reshape(rows, GRID, LANES) for f in range(halves)], axis=-1
        )
        at = pl.multiple_of(GRID * ((j + 1) % groups), GRID)
        pltpu.make_async_copy(outv.at[j], out_hbm.at[:, pl.ds(at, GRID), :], osem.at[j]).start()

    for copy in halo:
        copy.wait_send()
    for j in range(groups):
        for ref, sem in ((sec, send1), (outb, send2)):
            sent = ref.at[j, pl.ds(0, peers - 1)]
            pltpu.make_async_copy(sent, sent, sem.at[j]).wait()
        pltpu.make_async_copy(outv.at[j], outv.at[j], osem.at[j]).wait()


def local(
    image,
    bn_gain,
    bn_shift,
    w_expand,
    b_expand,
    w_depth,
    b_depth,
    w_project,
    b_project,
    attn_gain,
    attn_shift,
    w_qkv,
    w_out,
    rel_table,
    ffn_gain,
    ffn_shift,
    w_up,
    b_up,
    w_down,
    b_down,
):
    rows, cols, chans = image.shape
    strips = lax.axis_size("strip")
    col_groups = lax.axis_size("tile") // GRID
    heads = rel_table.shape[0]
    hidden = w_expand.shape[1]
    groups = cols // GRID
    peers = strips * GRID
    span = peers * PACK
    assert rows == strips * PACK and cols % GRID == 0 and hidden == w_up.shape[1]
    bf, f32 = jnp.bfloat16, jnp.float32
    vmem = pl.BlockSpec(memory_space=pltpu.VMEM)
    hbm = pl.BlockSpec(memory_space=pl.ANY)
    held = {7, 11, 12, 16, 18}
    unit = (groups, peers, PACK, chans)
    return pl.pallas_call(
        functools.partial(block_kernel, strips, col_groups, heads),
        out_shape=jax.ShapeDtypeStruct(image.shape, bf),
        in_specs=[hbm if i in held else vmem for i in range(20)],
        out_specs=hbm,
        scratch_shapes=[
            pltpu.VMEM(w_project.shape, bf),
            pltpu.VMEM(w_qkv.shape, bf),
            pltpu.VMEM(w_out.shape, bf),
            pltpu.VMEM(w_up.shape, bf),
            pltpu.VMEM(w_down.shape, bf),
            pltpu.VMEM((2, rows, chans), bf),
            pltpu.VMEM((2, strips, rows, chans), bf),
            pltpu.VMEM((2, cols, chans), bf),
            pltpu.VMEM((chans // LANES, (rows + 2) * (cols + 2 * PAD), LANES), f32),
            pltpu.VMEM((cols + 2, strips + 2, PACK, hidden), bf),
            pltpu.VMEM((strips + 2, PACK, hidden), bf),
            pltpu.VMEM((10, PACK, hidden), bf),
            pltpu.VMEM((strips, GRID, PACK, hidden), bf),
            pltpu.VMEM(unit, bf),
            pltpu.VMEM(unit, bf),
            pltpu.VMEM((heads, 256), f32),
            pltpu.VMEM((chans // LANES, GRID * GRID, 256), f32),
            pltpu.VMEM((span, span), bf),
            pltpu.VMEM((span, span), bf),
            pltpu.VMEM(unit, bf),
            pltpu.VMEM(unit, bf),
            pltpu.VMEM((chans // LANES, span, LANES), f32),
            pltpu.VMEM((groups, rows, GRID, chans), bf),
            pltpu.SemaphoreType.DMA((5,)),
            pltpu.SemaphoreType.DMA((groups,)),
            pltpu.SemaphoreType.DMA((groups,)),
            pltpu.SemaphoreType.DMA((groups,)),
            pltpu.SemaphoreType.DMA((groups,)),
            pltpu.SemaphoreType.DMA((3, 2)),
            pltpu.SemaphoreType.DMA((3, 2)),
            pltpu.SemaphoreType.DMA((groups,)),
        ],
        compiler_params=pltpu.CompilerParams(collective_id=0, has_side_effects=True),
    )(
        image,
        bn_gain.reshape(1, -1),
        bn_shift.reshape(1, -1),
        w_expand,
        b_expand.reshape(1, -1),
        w_depth,
        b_depth.reshape(1, -1),
        w_project,
        b_project.reshape(1, -1),
        attn_gain.reshape(1, -1),
        attn_shift.reshape(1, -1),
        w_qkv,
        w_out,
        rel_table,
        ffn_gain.reshape(1, -1),
        ffn_shift.reshape(1, -1),
        w_up,
        b_up.reshape(1, -1),
        w_down,
        b_down.reshape(1, -1),
    )


def solution(mesh):
    return jax.shard_map(
        local,
        mesh=mesh,
        in_specs=(P(("group", "strip"), "tile", None),) + (P(),) * 19,
        out_specs=P(("group", "strip"), "tile", None),
        check_vma=False,
    )
```

```python
import functools
import math

import jax
import jax.numpy as jnp
import numpy as np
from jax import lax
from jax.experimental import pallas as pl
from jax.experimental.pallas import tpu as pltpu
from jax.sharding import PartitionSpec as P

GRID = 8
EPSILON = 1e-05
LANES = 128
PACK = 16
MESH = pl.DeviceIdType.MESH

ROOT = math.sqrt(2.0 / math.pi)
SCALE = (ROOT * 0.044715) ** (1.0 / 3.0)
INNER = ROOT / SCALE
UNSCALE = 0.5 / SCALE
LOG2E = math.log2(math.e)


def scaled_gelu(z):
    return z + z * jnp.tanh(z * (z * z + INNER))


def layer_norm(inputs, norm_gain, norm_shift):
    center = jnp.mean(inputs, axis=-1, keepdims=True)
    spread = jnp.mean(jnp.square(inputs - center), axis=-1, keepdims=True)
    return (inputs - center) * lax.rsqrt(spread + EPSILON) * norm_gain + norm_shift


def dot(a, b):
    return jnp.dot(a, b, preferred_element_type=jnp.float32)


def dot_on(a, b, dims):
    return lax.dot_general(a, b, ((dims[:1], dims[1:]), ((), ())), preferred_element_type=jnp.float32)


def block_kernel(
    strips,
    col_groups,
    head_count,
    image_hbm,
    bng_ref,
    bns_ref,
    wexp_hbm,
    bexp_ref,
    wdep_ref,
    bdep_ref,
    wproj_hbm,
    bproj_ref,
    ag_ref,
    as_ref,
    wqkv_hbm,
    wout_hbm,
    table_ref,
    fg_ref,
    fs_ref,
    wup_hbm,
    bup_ref,
    wdown_hbm,
    bdown_ref,
    perm_hbm,
    rim_ref,
    corner_ref,
    out_hbm,
    image_ref,
    wexp_ref,
    perm_ref,
    wproj_ref,
    wqkv_ref,
    wout_ref,
    wup_ref,
    wdown_ref,
    cols_in,
    rows_in,
    u_s,
    e_s,
    wd_s,
    h_s,
    sec,
    arr,
    tab_s,
    bias_s,
    outb,
    sec2,
    outv,
    wsem,
    send1,
    recv1,
    send2,
    recv2,
    hsend,
    hrecv,
    osem,
):
    bf, f32 = jnp.bfloat16, jnp.float32
    rows, cols, chans = image_ref.shape
    hidden = wexp_ref.shape[1]
    groups = cols // GRID
    peers = strips * GRID
    kinds = strips + 2
    span = peers * PACK
    mine = GRID // strips
    places = GRID * GRID
    head_size = chans // head_count
    halves = chans // LANES
    half_heads = LANES // head_size
    me_s = lax.axis_index("strip")
    tile = lax.axis_index("tile")
    me_k = tile // col_groups
    within = tile % col_groups
    me_u = me_s * GRID + me_k

    def device(s, k):
        return {"strip": s, "tile": k * col_groups + within}

    loads = [
        pltpu.make_async_copy(src, dst, wsem.at[i])
        for i, (src, dst) in enumerate(
            (
                (image_hbm, image_ref),
                (perm_hbm, perm_ref),
                (wexp_hbm, wexp_ref),
                (wproj_hbm, wproj_ref),
                (wqkv_hbm, wqkv_ref),
                (wout_hbm, wout_ref),
                (wup_hbm, wup_ref),
                (wdown_hbm, wdown_ref),
            )
        )
    ]
    for copy in loads:
        copy.start()

    barrier = pltpu.get_barrier_semaphore()
    for m in range(1, peers):
        s, k = (me_s + m // GRID) % strips, (me_k + m) % GRID
        pl.semaphore_signal(barrier, inc=1, device_id=device(s, k), device_id_type=MESH)
    tiles = GRID * col_groups
    sides = ((tile + tiles - 1) % tiles, (tile + 1) % tiles)
    for t in sides:
        for s in range(strips):
            pl.semaphore_signal(
                barrier, inc=1, device_id={"strip": s, "tile": t}, device_id_type=MESH
            )

    def block(g):
        return image_ref[:, GRID * g : GRID * (g + 1), :].reshape(rows * GRID, chans)

    loads[0].wait()
    loads[1].wait()
    for g in range(groups):
        units = dot(perm_ref[0], block(g)).astype(bf)
        u_s[GRID * g + 1 : GRID * (g + 1) + 1, 1 : strips + 1] = units.reshape(
            GRID, strips, PACK, chans
        )

    pl.semaphore_wait(barrier, peers - 1 + 2 * strips)

    halo = []
    for i in range(2):
        halo.append(
            pltpu.make_async_remote_copy(
                image_ref.at[(rows - 1) * (1 - i)],
                rows_in.at[i],
                hsend.at[2, i],
                hrecv.at[2, i],
                device_id={"strip": (me_s + 1 + i * (strips - 2)) % strips, "tile": tile},
                device_id_type=MESH,
            )
        )
    for i in range(2):
        for s in range(strips):
            halo.append(
                pltpu.make_async_remote_copy(
                    u_s.at[1 + (cols - 1) * i, pl.ds(1, strips)],
                    cols_in.at[1 - i, me_s],
                    hsend.at[i, s],
                    hrecv.at[1 - i, me_s],
                    device_id={"strip": s, "tile": sides[i]},
                    device_id_type=MESH,
                )
            )
    for copy in halo:
        copy.start()

    row16 = lax.broadcasted_iota(jnp.int32, (PACK, LANES * 2), 0)
    bexp = jnp.broadcast_to(bexp_ref[...] * SCALE, (PACK, hidden)).astype(bf)
    top = jnp.where(row16 == 0, jnp.where(me_s == 0, 0.0, 1.0), 1.0).astype(bf)
    low = jnp.where(row16 == PACK - 1, jnp.where(me_s == strips - 1, 0.0, 1.0), 1.0).astype(bf)
    for tap in range(9):
        wd_s[tap] = jnp.broadcast_to(wdep_ref[tap : tap + 1, :] * 0.5, (GRID, hidden)).astype(bf)
    wd_s[9] = jnp.broadcast_to(bdep_ref[...] * SCALE, (GRID, hidden)).astype(bf)

    for i in range(2):
        pltpu.make_async_copy(rows_in.at[i], rows_in.at[i], hrecv.at[2, i]).wait()
    for g in range(groups):
        beyond = rows_in[:, GRID * g : GRID * (g + 1), :].reshape(2 * GRID, chans)
        units = (dot(perm_ref[1], block(g)) + dot(rim_ref[...], beyond)).astype(bf)
        units = units.reshape(GRID, 2, PACK, chans)
        at = slice(GRID * g + 1, GRID * (g + 1) + 1)
        u_s[at, 0] = units[:, 0]
        u_s[at, kinds - 1] = units[:, 1]

    bng = jnp.broadcast_to(bng_ref[...] * SCALE, (PACK, chans)).astype(bf)
    bns = jnp.broadcast_to(bns_ref[...] * SCALE, (PACK, chans)).astype(bf)
    loads[2].wait()

    def expand(first, batch, count):
        @pl.loop(0, count)
        def _(q):
            at = first + batch * q
            raw = u_s[pl.ds(at, batch)].reshape(batch * kinds, PACK, chans)
            lhs = (raw * bng + bns).reshape(batch * kinds * PACK, chans)
            for n in range(hidden // 256):
                lanes = slice(256 * n, 256 * (n + 1))
                z = dot(lhs, wexp_ref[:, lanes]).astype(bf).reshape(batch, kinds, PACK, 256)
                act = scaled_gelu(z + bexp[:, lanes])
                for kk in range(kinds):
                    a = act[:, kk]
                    if kk == 0:
                        a = a * top
                    if kk == kinds - 1:
                        a = a * low
                    e_s[pl.ds(at, batch), kk, :, :, lanes] = a.reshape(batch, 2, GRID, 256)

    expand(GRID, 2, 1)

    def first_send(j):
        sends = []
        for m in order:
            s, k = (me_s + m // GRID) % strips, (me_k + m) % GRID
            sends.append(
                pltpu.make_async_remote_copy(
                    sec.at[j, s * GRID + k],
                    arr.at[j, me_u],
                    send1.at[j],
                    recv1.at[j],
                    device_id=device(s, k),
                    device_id_type=MESH,
                )
            )
        return sends, pltpu.make_async_copy(sec.at[j, me_u], arr.at[j, me_u], recv1.at[j])

    def back_send(j):
        sends = []
        for m in order:
            s, k = (me_s + m // GRID) % strips, (me_k + m) % GRID
            sends.append(
                pltpu.make_async_remote_copy(
                    outb.at[j, s * GRID + k],
                    sec2.at[j, me_u],
                    send2.at[j],
                    recv2.at[j],
                    device_id=device(s, k),
                    device_id_type=MESH,
                )
            )
        return sends, pltpu.make_async_copy(outb.at[j, me_u], sec2.at[j, me_u], recv2.at[j])

    half = GRID // 2
    order = [m for m in range(1, peers)]
    order.sort(key=lambda m: abs(m % GRID - half))

    def flag(ok):
        return jnp.broadcast_to(jnp.where(ok, 1.0, 0.0), (GRID, hidden)).astype(bf)

    for j in range(groups):
        start = (GRID * (j + 1) + 2) % (cols + 2)
        if j == groups - 2:
            for i in range(2):
                for s in range(strips):
                    pltpu.make_async_copy(cols_in.at[i, s], cols_in.at[i, s], hrecv.at[i, s]).wait()
            for i in range(2):
                rim = cols_in[i].reshape(strips * rows, chans)
                units = dot(corner_ref[me_s], rim).astype(bf)
                u_s[(cols + 1) * i] = units.reshape(kinds, PACK, chans)
        expand(start, GRID // 2, 2)
        if j == groups - 2:
            ok = flag(tile < tiles - 1)
            for kk in range(kinds):
                e_s[cols + 1, kk] = e_s[cols + 1, kk] * ok
        if j == groups - 1:
            ok = flag(tile > 0)
            for kk in range(kinds):
                e_s[0, kk] = e_s[0, kk] * ok
        base = GRID * ((j + 1) % groups)

        @pl.loop(0, GRID // 2)
        def _(q):
            for n in range(hidden // 256):
                lanes = slice(256 * n, 256 * (n + 1))
                taps = [wd_s[t, :, lanes] for t in range(10)]
                for cc in range(2):
                    at = base + 2 * q + cc
                    for kk in range(strips):
                        acc = taps[9]
                        for a in range(3):
                            for b in range(3):
                                acc = acc + e_s[at + b, kk + a, :, :, lanes] * taps[3 * a + b]
                        h_s[kk, 2 * q + cc, :, :, lanes] = scaled_gelu(acc)

        if j == 0:
            loads[3].wait()
        skip = jnp.concatenate(
            [
                u_s[base + 1 : base + GRID + 1, kk + 1].reshape(GRID * PACK, chans)
                for kk in range(strips)
            ],
            axis=0,
        ).astype(f32)
        proj = dot(h_s[...].reshape(span, hidden), wproj_ref[...])
        out = skip + proj * UNSCALE + bproj_ref[...]
        sec[j] = out.astype(bf).reshape(peers, PACK, chans)
        sends, own = first_send(j)
        for copy in sends:
            copy.start()
        own.start()

    side = 2 * GRID - 1
    slot = 2 * GRID
    tab_s[...] = jnp.zeros_like(tab_s)
    tab_s[:, 0 : side * side] = table_ref[...] * LOG2E
    table = tab_s[...]
    lane = lax.broadcasted_iota(jnp.int32, (head_count, LANES), 1)
    sub = lax.broadcasted_iota(jnp.int32, (head_count, LANES), 0)
    in_pair = LANES // (half_heads * slot)
    for f in range(halves):
        keep = sub == half_heads * f + lane // slot % half_heads
        even, odd = [], []
        for d in range(side):
            x = pltpu.roll(table, (table.shape[1] - side * d) % table.shape[1], 1)[:, :LANES]
            x = jnp.where(lane < side, x, 0.0)
            n = slot
            while n < LANES:
                x = x + pltpu.roll(x, n, 1)
                n *= 2
            x = jnp.sum(jnp.where(keep, x, 0.0), axis=0, keepdims=True)
            x = jnp.broadcast_to(x, (GRID, LANES))
            x = pltpu.roll(x, LANES - (GRID - 1), 1, stride=1, stride_axis=0)
            even.append(x)
            odd.append(pltpu.roll(x, GRID, 1))
        lane8 = lax.broadcasted_iota(jnp.int32, (GRID, LANES), 1)
        first = lane8 % slot < GRID
        pair_of = lane8 // (half_heads * slot)
        tiles_by = []
        for d in range(side - 2 * in_pair + 1):
            tile_bias = jnp.where(first, even[d], odd[d + 1])
            for b in range(1, in_pair):
                more = jnp.where(first, even[d + 2 * b], odd[d + 2 * b + 1])
                tile_bias = jnp.where(pair_of == b, more, tile_bias)
            tiles_by.append(tile_bias)
        for g in range(GRID // 2 // in_pair):
            for r in range(GRID):
                bias_s[f, GRID * r : GRID * (r + 1), LANES * g : LANES * (g + 1)] = tiles_by[
                    GRID - 1 + 2 * in_pair * g - r
                ]

    lane16 = lax.broadcasted_iota(jnp.int32, (PACK, LANES), 1) // head_size
    masks = [jnp.where(lane16 == h, 1.0, 0.0).astype(bf) for h in range(half_heads)]
    loads[4].wait()
    loads[5].wait()
    pairs = places // PACK

    @pl.loop(0, groups)
    def _(j):
        pltpu.make_async_copy(arr.at[j], arr.at[j], recv1.at[j]).wait()
        x = arr[j].reshape(span, chans).astype(f32)
        normed = layer_norm(x, ag_ref[...], as_ref[...]).astype(bf)
        normed = dot(perm_ref[2], normed).astype(bf)
        q = (dot(normed, wqkv_ref[:, 0:chans]) * (head_size**-0.5 * LOG2E)).astype(bf)
        key = dot(normed, wqkv_ref[:, chans : 2 * chans]).astype(bf)
        val = dot(normed, wqkv_ref[:, 2 * chans :]).astype(bf)
        ctx = []
        for w in range(mine):
            parts = []
            for f in range(halves):
                at = (slice(places * w, places * (w + 1)), slice(LANES * f, LANES * (f + 1)))
                qh, kh, vh = q[at], key[at], val[at]
                qbd = jnp.concatenate(
                    [
                        qh[PACK * b : PACK * (b + 1)] * masks[h]
                        for b in range(pairs)
                        for h in range(half_heads)
                    ],
                    axis=0,
                )
                s = dot_on(kh, qbd, (1, 1)) + bias_s[f]
                e = jnp.exp2(s - jnp.max(s, axis=0, keepdims=True))
                p = (e * (1.0 / jnp.sum(e, axis=0, keepdims=True))).astype(bf)
                o = dot_on(p, vh, (0, 0)).reshape(pairs, half_heads, PACK, LANES)
                pick = o[:, 0]
                here = lax.broadcasted_iota(jnp.int32, pick.shape, 2) // head_size
                for h in range(1, half_heads):
                    pick = jnp.where(here == h, o[:, h], pick)
                parts.append(pick.reshape(places, LANES).astype(bf))
            ctx.append(jnp.concatenate(parts, axis=1))
        ctx = dot(perm_ref[3], jnp.concatenate(ctx, axis=0)).astype(bf)
        attended = (x + dot(ctx, wout_ref[...])).astype(bf)
        outb[j] = attended.reshape(peers, PACK, chans)
        sends, own = back_send(j)
        for copy in sends:
            copy.start()
        own.start()

    loads[6].wait()
    loads[7].wait()

    @pl.loop(0, groups)
    def _(j):
        pltpu.make_async_copy(sec2.at[j], sec2.at[j], recv2.at[j]).wait()
        x = sec2[j].reshape(span, chans).astype(f32)
        normed = layer_norm(x, fg_ref[...] * SCALE, fs_ref[...] * SCALE).astype(bf)
        bup = jnp.broadcast_to(bup_ref[...] * SCALE, (PACK, hidden)).astype(bf)
        for n in range(hidden // 256):
            lanes = slice(256 * n, 256 * (n + 1))
            z = dot(normed, wup_ref[:, lanes]).astype(bf).reshape(peers, PACK, 256)
            act = scaled_gelu(z + bup[:, lanes])
            h_s[:, :, :, :, lanes] = act.reshape(strips, GRID, 2, GRID, 256)
        res = dot(h_s[...].reshape(span, hidden), wdown_ref[...]) * UNSCALE
        res = x + res + bdown_ref[...]
        outv[j] = dot(perm_ref[4], res.astype(bf)).astype(bf).reshape(rows, GRID, chans)
        at = pl.multiple_of(GRID * ((j + 1) % groups), GRID)
        pltpu.make_async_copy(outv.at[j], out_hbm.at[:, pl.ds(at, GRID), :], osem.at[j]).start()

    for copy in halo:
        copy.wait_send()
    for j in range(groups):
        for ref, sem in ((sec, send1), (outb, send2)):
            sent = ref.at[j, pl.ds(0, peers - 1)]
            pltpu.make_async_copy(sent, sent, sem.at[j]).wait()
        pltpu.make_async_copy(outv.at[j], outv.at[j], osem.at[j]).wait()


def permutations(strips, rows, grid_rows):
    span = rows * GRID
    mine = GRID // strips
    out = np.zeros((5, span, span), np.float32)
    rim = np.zeros((span, 2 * GRID), np.float32)
    corner = np.zeros((strips, (strips + 2) * PACK, strips * rows), np.float32)
    for c in range(GRID):
        for p in range(PACK):
            for k in range(strips):
                row = (strips * p + k) * GRID + c
                out[0, (c * strips + k) * PACK + p, row] = 1
                out[4, row, (k * GRID + c) * PACK + p] = 1
            if p > 0:
                out[1, (2 * c) * PACK + p, (strips * p - 1) * GRID + c] = 1
            else:
                rim[(2 * c) * PACK + p, c] = 1
            if p < PACK - 1:
                out[1, (2 * c + 1) * PACK + p, strips * (p + 1) * GRID + c] = 1
            else:
                rim[(2 * c + 1) * PACK + p, GRID + c] = 1
    for s in range(strips):
        for k in range(strips + 2):
            for p in range(PACK):
                row = s * rows + strips * p + k - 1
                if 0 <= row < strips * rows:
                    far, within = row // rows, row % rows
                    at = far * rows + within % strips * PACK + within // strips
                    corner[s, k * PACK + p, at] = 1
        for k in range(GRID):
            for p in range(PACK):
                token = (s * GRID + k) * PACK + p
                place = p % mine * GRID * GRID + (grid_rows * s + p // mine) * GRID + k
                out[2, place, token] = 1
                out[3, token, place] = 1
    return tuple(jnp.asarray(a, jnp.bfloat16) for a in (out, rim, corner))


def local(
    image,
    bn_gain,
    bn_shift,
    w_expand,
    b_expand,
    w_depth,
    b_depth,
    w_project,
    b_project,
    attn_gain,
    attn_shift,
    w_qkv,
    w_out,
    rel_table,
    ffn_gain,
    ffn_shift,
    w_up,
    b_up,
    w_down,
    b_down,
):
    rows, cols, chans = image.shape
    strips = lax.axis_size("strip")
    col_groups = lax.axis_size("tile") // GRID
    heads = rel_table.shape[0]
    hidden = w_expand.shape[1]
    groups = cols // GRID
    peers = strips * GRID
    span = peers * PACK
    assert rows == strips * PACK and cols % GRID == 0 and hidden == w_up.shape[1]
    bf, f32 = jnp.bfloat16, jnp.float32
    vmem = pl.BlockSpec(memory_space=pltpu.VMEM)
    hbm = pl.BlockSpec(memory_space=pl.ANY)
    held = {0, 3, 7, 11, 12, 16, 18, 20}
    perm, rim, corner = permutations(strips, rows, rows // GRID)
    unit = (groups, peers, PACK, chans)
    return pl.pallas_call(
        functools.partial(block_kernel, strips, col_groups, heads),
        out_shape=jax.ShapeDtypeStruct(image.shape, bf),
        in_specs=[hbm if i in held else vmem for i in range(23)],
        out_specs=hbm,
        scratch_shapes=[
            pltpu.VMEM(image.shape, bf),
            pltpu.VMEM(w_expand.shape, bf),
            pltpu.VMEM(perm.shape, bf),
            pltpu.VMEM(w_project.shape, bf),
            pltpu.VMEM(w_qkv.shape, bf),
            pltpu.VMEM(w_out.shape, bf),
            pltpu.VMEM(w_up.shape, bf),
            pltpu.VMEM(w_down.shape, bf),
            pltpu.VMEM((2, strips, strips, PACK, chans), bf),
            pltpu.VMEM((2, cols, chans), bf),
            pltpu.VMEM((cols + 2, strips + 2, PACK, chans), bf),
            pltpu.VMEM((cols + 2, strips + 2, 2, GRID, hidden), bf),
            pltpu.VMEM((10, GRID, hidden), bf),
            pltpu.VMEM((strips, GRID, 2, GRID, hidden), bf),
            pltpu.VMEM(unit, bf),
            pltpu.VMEM(unit, bf),
            pltpu.VMEM((heads, 256), f32),
            pltpu.VMEM((chans // LANES, GRID * GRID, 256), f32),
            pltpu.VMEM(unit, bf),
            pltpu.VMEM(unit, bf),
            pltpu.VMEM((groups, rows, GRID, chans), bf),
            pltpu.SemaphoreType.DMA((8,)),
            pltpu.SemaphoreType.DMA((groups,)),
            pltpu.SemaphoreType.DMA((groups,)),
            pltpu.SemaphoreType.DMA((groups,)),
            pltpu.SemaphoreType.DMA((groups,)),
            pltpu.SemaphoreType.DMA((3, 2)),
            pltpu.SemaphoreType.DMA((3, 2)),
            pltpu.SemaphoreType.DMA((groups,)),
        ],
        compiler_params=pltpu.CompilerParams(collective_id=0, has_side_effects=True),
    )(
        image,
        bn_gain.reshape(1, -1),
        bn_shift.reshape(1, -1),
        w_expand,
        b_expand.reshape(1, -1),
        w_depth,
        b_depth.reshape(1, -1),
        w_project,
        b_project.reshape(1, -1),
        attn_gain.reshape(1, -1),
        attn_shift.reshape(1, -1),
        w_qkv,
        w_out,
        rel_table,
        ffn_gain.reshape(1, -1),
        ffn_shift.reshape(1, -1),
        w_up,
        b_up.reshape(1, -1),
        w_down,
        b_down.reshape(1, -1),
        perm,
        rim,
        corner,
    )


def solution(mesh):
    return jax.shard_map(
        local,
        mesh=mesh,
        in_specs=(P(("group", "strip"), "tile", None),) + (P(),) * 19,
        out_specs=P(("group", "strip"), "tile", None),
        check_vma=False,
    )
```

```python
import functools
import math

import jax
import jax.numpy as jnp
import numpy as np
from jax import lax
from jax.experimental import pallas as pl
from jax.experimental.pallas import tpu as pltpu
from jax.sharding import PartitionSpec as P

GRID = 8
EPSILON = 1e-05
LANES = 128
PACK = 16
OPERANDS = 23
REACH = 2
MESH = pl.DeviceIdType.MESH

ROOT = math.sqrt(2.0 / math.pi)
SCALE = (ROOT * 0.044715) ** (1.0 / 3.0)
INNER = ROOT / SCALE
UNSCALE = 0.5 / SCALE
LOG2E = math.log2(math.e)


def scaled_gelu(z):
    return z + z * jnp.tanh(z * (z * z + INNER))


def layer_norm(inputs, norm_gain, norm_shift):
    center = jnp.mean(inputs, axis=-1, keepdims=True)
    spread = jnp.mean(jnp.square(inputs - center), axis=-1, keepdims=True)
    return (inputs - center) * lax.rsqrt(spread + EPSILON) * norm_gain + norm_shift


def dot(a, b):
    return jnp.dot(a, b, preferred_element_type=jnp.float32)


def dot_on(a, b, dims):
    return lax.dot_general(a, b, ((dims[:1], dims[1:]), ((), ())), preferred_element_type=jnp.float32)


def block_kernel(
    strips,
    col_groups,
    head_count,
    *refs,
):
    operands, out_ref, held = refs[:OPERANDS], refs[OPERANDS], refs[OPERANDS + 1 : 2 * OPERANDS + 1]
    (
        image_ref,
        bng_ref,
        bns_ref,
        wexp_ref,
        bexp_ref,
        wdep_ref,
        bdep_ref,
        wproj_ref,
        bproj_ref,
        ag_ref,
        as_ref,
        wqkv_ref,
        wout_ref,
        table_ref,
        fg_ref,
        fs_ref,
        wup_ref,
        bup_ref,
        wdown_ref,
        bdown_ref,
        perm_ref,
        rim_ref,
        corner_ref,
    ) = held
    (
        cols_in,
        rows_in,
        u_s,
        e_s,
        wd_s,
        h_s,
        sec,
        arr,
        tab_s,
        bias_s,
        outb,
        sec2,
        wsem,
        send1,
        recv1,
        send2,
        recv2,
        hsend,
        hrecv,
        relay,
    ) = refs[2 * OPERANDS + 1 :]
    bf, f32 = jnp.bfloat16, jnp.float32
    rows, cols, chans = image_ref.shape
    hidden = wexp_ref.shape[1]
    groups = cols // GRID
    peers = strips * GRID
    kinds = strips + 2
    span = peers * PACK
    mine = GRID // strips
    places = GRID * GRID
    head_size = chans // head_count
    halves = chans // LANES
    half_heads = LANES // head_size
    me_s = lax.axis_index("strip")
    tile = lax.axis_index("tile")
    me_k = tile // col_groups
    within = tile % col_groups
    me_u = me_s * GRID + me_k

    def device(s, k):
        return {"strip": s, "tile": k * col_groups + within}

    half = GRID // 2
    tiles = GRID * col_groups
    loads = [
        pltpu.make_async_copy(src, dst, wsem.at[i])
        for i, (src, dst) in enumerate(zip(operands, held))
    ]
    early = (0, 20, 3, 1, 2, 4)
    for i in early[:2]:
        loads[i].start()

    barrier = pltpu.get_barrier_semaphore()
    for s in range(1, strips):
        pl.semaphore_signal(
            barrier, inc=1, device_id=device((me_s + s) % strips, me_k), device_id_type=MESH
        )
    expected = strips - 1
    near = [d for r in range(REACH, 0, -1) for d in (r, -r)]
    greet = [(me_k + d >= 0) & (me_k + d < GRID) for d in near]
    greet = [(ok, (me_k + d) * col_groups + within) for d, ok in zip(near, greet)]
    rim_sides = ((tile > 0, tile - 1), (tile < tiles - 1, tile + 1))
    for ok, t in greet + list(rim_sides):
        expected = expected + jnp.where(ok, strips, 0)

        @pl.when(ok)
        def _():
            for s in range(strips):
                pl.semaphore_signal(
                    barrier, inc=1, device_id={"strip": s, "tile": t}, device_id_type=MESH
                )

    for i in early[2:]:
        loads[i].start()
    for i in range(OPERANDS):
        if i not in early:
            loads[i].start()

    def spread(stage):
        for i, d in enumerate((REACH, -REACH)):

            @pl.when((me_k + d >= 0) & (me_k + d < GRID))
            def _():
                pl.semaphore_signal(
                    relay.at[stage, i],
                    inc=1,
                    device_id=device(me_s, me_k + d),
                    device_id_type=MESH,
                )

    def heard(stage):
        for i, d in enumerate((-REACH, REACH)):

            @pl.when((me_k + d >= 0) & (me_k + d < GRID))
            def _():
                pl.semaphore_wait(relay.at[stage, i], 1)

    def block(g):
        return image_ref[:, GRID * g : GRID * (g + 1), :].reshape(rows * GRID, chans)

    loads[0].wait()
    loads[20].wait()

    def permute(g):
        tokens = block(g)
        at = slice(GRID * g + 1, GRID * (g + 1) + 1)
        units = dot(perm_ref[0], tokens).astype(bf)
        u_s[at, 0:strips] = units.reshape(GRID, strips, PACK, chans)
        units = dot(perm_ref[1], tokens).astype(bf)
        u_s[at, strips:kinds] = units.reshape(GRID, 2, PACK, chans)

    for g in range(min(3, groups)):
        permute(g)

    pl.semaphore_wait(barrier, expected)
    spread(0)

    halo = []
    for i in range(2):
        halo.append(
            pltpu.make_async_remote_copy(
                image_ref.at[(rows - 1) * (1 - i)],
                rows_in.at[i],
                hsend.at[2, i],
                hrecv.at[2, i],
                device_id={"strip": (me_s + 1 + i * (strips - 2)) % strips, "tile": tile},
                device_id_type=MESH,
            )
        )
    for copy in halo:
        copy.start()
    for g in range(3, groups):
        permute(g)
    rims = []
    for i, (ok, t) in enumerate(rim_sides):
        for s in range(strips):
            rims.append(
                (
                    ok,
                    pltpu.make_async_remote_copy(
                        u_s.at[1 + (cols - 1) * i, pl.ds(0, strips)],
                        cols_in.at[1 - i, me_s],
                        hsend.at[i, s],
                        hrecv.at[1 - i, me_s],
                        device_id={"strip": s, "tile": t},
                        device_id_type=MESH,
                    ),
                )
            )
    for ok, copy in rims:

        @pl.when(ok)
        def _():
            copy.start()

    for i in early[2:]:
        loads[i].wait()
    row16 = lax.broadcasted_iota(jnp.int32, (PACK, LANES * 2), 0)
    bexp = jnp.broadcast_to(bexp_ref[...] * SCALE, (PACK, hidden)).astype(bf)
    top = jnp.where(row16 == 0, jnp.where(me_s == 0, 0.0, 1.0), 1.0).astype(bf)
    low = jnp.where(row16 == PACK - 1, jnp.where(me_s == strips - 1, 0.0, 1.0), 1.0).astype(bf)
    bng = jnp.broadcast_to(bng_ref[...] * SCALE, (PACK, chans)).astype(bf)
    bns = jnp.broadcast_to(bns_ref[...] * SCALE, (PACK, chans)).astype(bf)

    def expand(at, batch, kind, count):
        raw = u_s[pl.ds(at, batch), kind : kind + count].reshape(batch * count, PACK, chans)
        lhs = (raw * bng + bns).reshape(batch * count * PACK, chans)
        for n in range(hidden // 256):
            lanes = slice(256 * n, 256 * (n + 1))
            z = dot(lhs, wexp_ref[:, lanes]).astype(bf).reshape(batch, count, PACK, 256)
            act = scaled_gelu(z + bexp[:, lanes])
            for c in range(count):
                a = act[:, c]
                if kind + c == strips:
                    a = a * top
                if kind + c == strips + 1:
                    a = a * low
                e_s[pl.ds(at, batch), kind + c, :, :, lanes] = a.reshape(batch, 2, GRID, 256)

    far = (me_k // half + 1) % 2
    batches = ((GRID + half * far, half + 2), (GRID + (half + 2) * (1 - far), half))
    for at, batch in batches:
        expand(at, batch, 0, strips)
    for i in (5, 6):
        loads[i].wait()
    for tap in range(9):
        wd_s[tap] = jnp.broadcast_to(wdep_ref[tap : tap + 1, :] * 0.5, (GRID, hidden)).astype(bf)
    wd_s[9] = jnp.broadcast_to(bdep_ref[...] * SCALE, (GRID, hidden)).astype(bf)
    heard(0)
    spread(1)
    for i in range(2):
        pltpu.make_async_copy(rows_in.at[i], rows_in.at[i], hrecv.at[2, i]).wait()
    loads[21].wait()

    def add_rim(g):
        beyond = rows_in[:, GRID * g : GRID * (g + 1), :].reshape(2 * GRID, chans)
        units = dot(rim_ref[...], beyond).astype(bf).reshape(GRID, 2, PACK, chans)
        at = slice(GRID * g + 1, GRID * (g + 1) + 1)
        u_s[at, strips:kinds] = u_s[at, strips:kinds] + units

    for g in range(min(3, groups)):
        add_rim(g)
    heard(1)
    spread(2)

    def first_send(j, h, own):
        sends = []
        for m in range(own, strips * half):
            s, k = (me_s + m // half) % strips, half * h + (me_k + m) % half
            sends.append(
                pltpu.make_async_remote_copy(
                    sec.at[j, s * GRID + k],
                    arr.at[j, me_u],
                    send1.at[j],
                    recv1.at[j],
                    device_id=device(s, k),
                    device_id_type=MESH,
                )
            )
        return sends

    def first_own(j):
        return pltpu.make_async_copy(sec.at[j, me_u], arr.at[j, me_u], recv1.at[j])

    def back_send(j):
        sends = []
        for m in order:
            s, k = (me_s + m // GRID) % strips, (me_k + m) % GRID
            sends.append(
                pltpu.make_async_remote_copy(
                    outb.at[j, s * GRID + k],
                    sec2.at[j, me_u],
                    send2.at[j],
                    recv2.at[j],
                    device_id=device(s, k),
                    device_id_type=MESH,
                )
            )
        return sends, pltpu.make_async_copy(outb.at[j, me_u], sec2.at[j, me_u], recv2.at[j])

    order = [m for m in range(1, peers)]
    order.sort(key=lambda m: abs(m % GRID - half))

    def flag(ok):
        return jnp.broadcast_to(jnp.where(ok, 1.0, 0.0), (GRID, hidden)).astype(bf)

    for j in range(groups):
        start = (GRID * (j + 1) + 2) % (cols + 2)
        if j == 1:
            for g in range(3, groups):
                add_rim(g)
        if j == groups - 2:
            loads[22].wait()
            for i, (ok, _) in enumerate(rim_sides):

                @pl.when(ok)
                def _():
                    for s in range(strips):
                        ref = cols_in.at[i, s]
                        pltpu.make_async_copy(ref, ref, hrecv.at[i, s]).wait()

                @pl.when(jnp.logical_not(ok))
                def _():
                    cols_in[i] = jnp.zeros(cols_in.shape[1:], bf)

            for i in range(2):
                rim = cols_in[i].reshape(strips * rows, chans)
                units = dot(corner_ref[me_s], rim).astype(bf)
                u_s[(cols + 1) * i] = units.reshape(kinds, PACK, chans)
        if j > 0:

            @pl.loop(0, 2)
            def _(q):
                expand(start + half * q, half, 0, kinds)

        if j == groups - 2:
            ok = flag(tile < tiles - 1)
            for kk in range(kinds):
                e_s[cols + 1, kk] = e_s[cols + 1, kk] * ok
        if j == groups - 1:
            ok = flag(tile > 0)
            for kk in range(kinds):
                e_s[0, kk] = e_s[0, kk] * ok
        base = GRID * ((j + 1) % groups)

        for step in range(2):
            h = (far + step) % 2
            if j == 0:
                expand(*batches[step], strips, 2)

            @pl.loop(0, half // 2)
            def _(q):
                for n in range(hidden // 256):
                    lanes = slice(256 * n, 256 * (n + 1))
                    taps = [wd_s[t, :, lanes] for t in range(10)]
                    for cc in range(2):
                        at = base + half * h + 2 * q + cc
                        for kk in range(strips):
                            acc = taps[9]
                            for a in range(3):
                                kind = (kk + a - 1, strips, strips + 1)[
                                    1 if kk + a == 0 else 2 if kk + a == strips + 1 else 0
                                ]
                                for b in range(3):
                                    acc = acc + e_s[at + b, kind, :, :, lanes] * taps[3 * a + b]
                            h_s[kk, 2 * q + cc, :, :, lanes] = scaled_gelu(acc)

            if j == 0 and step == 0:
                loads[7].wait()
                loads[8].wait()
            first = base + half * h + 1
            skip = jnp.concatenate(
                [u_s[pl.ds(first, half), kk].reshape(half * PACK, chans) for kk in range(strips)],
                axis=0,
            ).astype(f32)
            act = h_s[:, 0:half].reshape(strips * half * PACK, hidden)
            out = skip + dot(act, wproj_ref[...]) * UNSCALE + bproj_ref[...]
            out = out.astype(bf).reshape(strips, half, PACK, chans)
            for s in range(strips):
                sec[j, pl.ds(s * GRID + half * h, half)] = out[s]
            if j == 0 and step == 0:
                heard(2)
            for copy in first_send(j, h, step):
                copy.start()
            if step == 1:
                first_own(j).start()

    side = 2 * GRID - 1
    slot = 2 * GRID
    tab_s[...] = jnp.zeros_like(tab_s)
    loads[13].wait()
    tab_s[:, 0 : side * side] = table_ref[...] * LOG2E
    table = tab_s[...]
    lane = lax.broadcasted_iota(jnp.int32, (head_count, LANES), 1)
    sub = lax.broadcasted_iota(jnp.int32, (head_count, LANES), 0)
    in_pair = LANES // (half_heads * slot)
    for f in range(halves):
        keep = sub == half_heads * f + lane // slot % half_heads
        even, odd = [], []
        for d in range(side):
            x = pltpu.roll(table, (table.shape[1] - side * d) % table.shape[1], 1)[:, :LANES]
            x = jnp.where(lane < side, x, 0.0)
            n = slot
            while n < LANES:
                x = x + pltpu.roll(x, n, 1)
                n *= 2
            x = jnp.sum(jnp.where(keep, x, 0.0), axis=0, keepdims=True)
            x = jnp.broadcast_to(x, (GRID, LANES))
            x = pltpu.roll(x, LANES - (GRID - 1), 1, stride=1, stride_axis=0)
            even.append(x)
            odd.append(pltpu.roll(x, GRID, 1))
        lane8 = lax.broadcasted_iota(jnp.int32, (GRID, LANES), 1)
        first = lane8 % slot < GRID
        pair_of = lane8 // (half_heads * slot)
        tiles_by = []
        for d in range(side - 2 * in_pair + 1):
            tile_bias = jnp.where(first, even[d], odd[d + 1])
            for b in range(1, in_pair):
                more = jnp.where(first, even[d + 2 * b], odd[d + 2 * b + 1])
                tile_bias = jnp.where(pair_of == b, more, tile_bias)
            tiles_by.append(tile_bias)
        for g in range(GRID // 2 // in_pair):
            for r in range(GRID):
                bias_s[f, GRID * r : GRID * (r + 1), LANES * g : LANES * (g + 1)] = tiles_by[
                    GRID - 1 + 2 * in_pair * g - r
                ]

    lane16 = lax.broadcasted_iota(jnp.int32, (PACK, LANES), 1) // head_size
    masks = [jnp.where(lane16 == h, 1.0, 0.0).astype(bf) for h in range(half_heads)]
    for i in (9, 10, 11, 12):
        loads[i].wait()
    pairs = places // PACK

    @pl.loop(0, groups)
    def _(j):
        pltpu.make_async_copy(arr.at[j], arr.at[j], recv1.at[j]).wait()
        x = arr[j].reshape(span, chans).astype(f32)
        normed = layer_norm(x, ag_ref[...], as_ref[...]).astype(bf)
        normed = dot(perm_ref[2], normed).astype(bf)
        q = (dot(normed, wqkv_ref[:, 0:chans]) * (head_size**-0.5 * LOG2E)).astype(bf)
        key = dot(normed, wqkv_ref[:, chans : 2 * chans]).astype(bf)
        val = dot(normed, wqkv_ref[:, 2 * chans :]).astype(bf)
        ctx = []
        for w in range(mine):
            parts = []
            for f in range(halves):
                at = (slice(places * w, places * (w + 1)), slice(LANES * f, LANES * (f + 1)))
                qh, kh, vh = q[at], key[at], val[at]
                qbd = jnp.concatenate(
                    [
                        qh[PACK * b : PACK * (b + 1)] * masks[h]
                        for b in range(pairs)
                        for h in range(half_heads)
                    ],
                    axis=0,
                )
                s = dot_on(kh, qbd, (1, 1)) + bias_s[f]
                e = jnp.exp2(s - jnp.max(s, axis=0, keepdims=True))
                p = (e * (1.0 / jnp.sum(e, axis=0, keepdims=True))).astype(bf)
                o = dot_on(p, vh, (0, 0)).reshape(pairs, half_heads, PACK, LANES)
                pick = o[:, 0]
                here = lax.broadcasted_iota(jnp.int32, pick.shape, 2) // head_size
                for h in range(1, half_heads):
                    pick = jnp.where(here == h, o[:, h], pick)
                parts.append(pick.reshape(places, LANES).astype(bf))
            ctx.append(jnp.concatenate(parts, axis=1))
        ctx = dot(perm_ref[3], jnp.concatenate(ctx, axis=0)).astype(bf)
        attended = (x + dot(ctx, wout_ref[...])).astype(bf)
        outb[j] = attended.reshape(peers, PACK, chans)
        sends, own = back_send(j)
        for copy in sends:
            copy.start()
        own.start()

    for i in (14, 15, 16, 17, 18, 19):
        loads[i].wait()

    @pl.loop(0, groups)
    def _(j):
        pltpu.make_async_copy(sec2.at[j], sec2.at[j], recv2.at[j]).wait()
        x = sec2[j].reshape(span, chans).astype(f32)
        normed = layer_norm(x, fg_ref[...] * SCALE, fs_ref[...] * SCALE).astype(bf)
        bup = jnp.broadcast_to(bup_ref[...] * SCALE, (PACK, hidden)).astype(bf)
        for n in range(hidden // 256):
            lanes = slice(256 * n, 256 * (n + 1))
            z = dot(normed, wup_ref[:, lanes]).astype(bf).reshape(peers, PACK, 256)
            act = scaled_gelu(z + bup[:, lanes])
            h_s[:, :, :, :, lanes] = act.reshape(strips, GRID, 2, GRID, 256)
        res = dot(h_s[...].reshape(span, hidden), wdown_ref[...]) * UNSCALE
        res = x + res + bdown_ref[...]
        final = dot(perm_ref[4], res.astype(bf)).astype(bf).reshape(rows, GRID, chans)
        at = pl.multiple_of(GRID * ((j + 1) % groups), GRID)
        out_ref[:, pl.ds(at, GRID), :] = final

    for copy in halo:
        copy.wait_send()
    for ok, copy in rims:

        @pl.when(ok)
        def _():
            copy.wait_send()

    for j in range(groups):
        for ref, sem in ((sec, send1), (outb, send2)):
            sent = ref.at[j, pl.ds(0, peers - 1)]
            pltpu.make_async_copy(sent, sent, sem.at[j]).wait()


def permutations(strips, rows, grid_rows):
    span = rows * GRID
    mine = GRID // strips
    out = np.zeros((5, span, span), np.float32)
    rim = np.zeros((span, 2 * GRID), np.float32)
    corner = np.zeros((strips, (strips + 2) * PACK, strips * rows), np.float32)
    for c in range(GRID):
        for p in range(PACK):
            for k in range(strips):
                row = (strips * p + k) * GRID + c
                out[0, (c * strips + k) * PACK + p, row] = 1
                out[4, row, (k * GRID + c) * PACK + p] = 1
            if p > 0:
                out[1, (2 * c) * PACK + p, (strips * p - 1) * GRID + c] = 1
            else:
                rim[(2 * c) * PACK + p, c] = 1
            if p < PACK - 1:
                out[1, (2 * c + 1) * PACK + p, strips * (p + 1) * GRID + c] = 1
            else:
                rim[(2 * c + 1) * PACK + p, GRID + c] = 1
    for s in range(strips):
        for k in range(strips + 2):
            shift = {strips: -1, strips + 1: strips}.get(k, k)
            for p in range(PACK):
                row = s * rows + strips * p + shift
                if 0 <= row < strips * rows:
                    far, within = row // rows, row % rows
                    at = far * rows + within % strips * PACK + within // strips
                    corner[s, k * PACK + p, at] = 1
        for k in range(GRID):
            for p in range(PACK):
                token = (s * GRID + k) * PACK + p
                place = p % mine * GRID * GRID + (grid_rows * s + p // mine) * GRID + k
                out[2, place, token] = 1
                out[3, token, place] = 1
    return tuple(jnp.asarray(a, jnp.bfloat16) for a in (out, rim, corner))


def local(
    image,
    bn_gain,
    bn_shift,
    w_expand,
    b_expand,
    w_depth,
    b_depth,
    w_project,
    b_project,
    attn_gain,
    attn_shift,
    w_qkv,
    w_out,
    rel_table,
    ffn_gain,
    ffn_shift,
    w_up,
    b_up,
    w_down,
    b_down,
):
    rows, cols, chans = image.shape
    strips = lax.axis_size("strip")
    col_groups = lax.axis_size("tile") // GRID
    heads = rel_table.shape[0]
    hidden = w_expand.shape[1]
    groups = cols // GRID
    peers = strips * GRID
    span = peers * PACK
    assert rows == strips * PACK and cols % GRID == 0 and hidden == w_up.shape[1]
    bf, f32 = jnp.bfloat16, jnp.float32
    vmem = pl.BlockSpec(memory_space=pltpu.VMEM)
    hbm = pl.BlockSpec(memory_space=pl.ANY)
    perm, rim, corner = permutations(strips, rows, rows // GRID)
    unit = (groups, peers, PACK, chans)
    operands = (
        image,
        bn_gain.reshape(1, -1),
        bn_shift.reshape(1, -1),
        w_expand,
        b_expand.reshape(1, -1),
        w_depth,
        b_depth.reshape(1, -1),
        w_project,
        b_project.reshape(1, -1),
        attn_gain.reshape(1, -1),
        attn_shift.reshape(1, -1),
        w_qkv,
        w_out,
        rel_table,
        ffn_gain.reshape(1, -1),
        ffn_shift.reshape(1, -1),
        w_up,
        b_up.reshape(1, -1),
        w_down,
        b_down.reshape(1, -1),
        perm,
        rim,
        corner,
    )
    call = pl.pallas_call(
        functools.partial(block_kernel, strips, col_groups, heads),
        out_shape=pltpu.VMEM(image.shape, bf),
        in_specs=[hbm] * OPERANDS,
        out_specs=vmem,
        scratch_shapes=[
            *(pltpu.VMEM(a.shape, a.dtype) for a in operands),
            pltpu.VMEM((2, strips, strips, PACK, chans), bf),
            pltpu.VMEM((2, cols, chans), bf),
            pltpu.VMEM((cols + 2, strips + 2, PACK, chans), bf),
            pltpu.VMEM((cols + 2, strips + 2, 2, GRID, hidden), bf),
            pltpu.VMEM((10, GRID, hidden), bf),
            pltpu.VMEM((strips, GRID, 2, GRID, hidden), bf),
            pltpu.VMEM(unit, bf),
            pltpu.VMEM(unit, bf),
            pltpu.VMEM((heads, 256), f32),
            pltpu.VMEM((chans // LANES, GRID * GRID, 256), f32),
            pltpu.VMEM(unit, bf),
            pltpu.VMEM(unit, bf),
            pltpu.SemaphoreType.DMA((OPERANDS,)),
            pltpu.SemaphoreType.DMA((groups,)),
            pltpu.SemaphoreType.DMA((groups,)),
            pltpu.SemaphoreType.DMA((groups,)),
            pltpu.SemaphoreType.DMA((groups,)),
            pltpu.SemaphoreType.DMA((3, 2)),
            pltpu.SemaphoreType.DMA((3, 2)),
            pltpu.SemaphoreType.REGULAR((-(-(GRID - 1) // REACH) - 1, 2)),
        ],
        compiler_params=pltpu.CompilerParams(collective_id=0, has_side_effects=True),
    )
    return call(*operands)


def solution(mesh):
    return jax.shard_map(
        local,
        mesh=mesh,
        in_specs=(P(("group", "strip"), "tile", None),) + (P(),) * 19,
        out_specs=P(("group", "strip"), "tile", None),
        check_vma=False,
    )
```
